32 devices in a mesh: row: 4 (over y, x), col: 8 (over z, core).
Axes of the slice: x: 2, y: 2, z: 4, core: 2. Of those that a mesh axis runs over, the one named last changes fastest.
Arguments:
- residual_input: bfloat16 [1024, 2048], P('row', 'col'), may hold values from -6 to 6
- embeddings: bfloat16 [1024, 2048], P('row', 'col'), may hold values from -6 to 6
- sequence_numbers: int32 [4, 256], P('row'), may hold values from 0 to 3, never falling along the last dimension, each value on 1 to 128 neighbouring positions
- attention_norm_gain: float32 [2, 2048], P(None, 'col'), may hold values from 0.5 to 1.5
- query_matrix: bfloat16 [2, 2048, 4096], P(None, 'row', 'col'), may hold values from -0.09375 to 0.09375
- key_matrix: bfloat16 [2, 2048, 4096], P(None, 'row', 'col'), may hold values from -0.09375 to 0.09375
- value_matrix: bfloat16 [2, 2048, 4096], P(None, 'row', 'col'), may hold values from -0.09375 to 0.09375
- attention_output_matrix: bfloat16 [4096, 2, 2048], P('col', None, 'row'), may hold values from -0.1875 to 0.1875
- feedforward_norm_gain: float32 [2, 2048], P(None, 'col'), may hold values from 0.5 to 1.5
- gate_matrix: bfloat16 [2, 2048, 8192], P(None, 'row', 'col'), may hold values from -0.09375 to 0.09375
- up_matrix: bfloat16 [2, 2048, 8192], P(None, 'row', 'col'), may hold values from -0.09375 to 0.09375
- adapter_down: bfloat16 [2, 2048, 128], P(None, 'row', 'col'), may hold values from -0.09375 to 0.09375
- adapter_gate: bfloat16 [128, 8192], P('row', 'col'), may hold values from -0.5 to 0.5
- adapter_up: bfloat16 [128, 8192], P('row', 'col'), may hold values from -0.5 to 0.5
- down_matrix: bfloat16 [8192, 2, 2048], P('col', None, 'row'), may hold values from -0.0625 to 0.0625
- projection_matrix: bfloat16 [2, 2048, 2048], P(None, 'col', 'row'), may hold values from -0.09375 to 0.09375
- mixer_norm_gain: float32 [2048], P('col'), may hold values from 0.5 to 1.5
- mixer_gate_matrix: bfloat16 [2048, 4096], P('row', 'col'), may hold values from -0.125 to 0.125
- mixer_input_matrix: bfloat16 [2048, 4096], P('row', 'col'), may hold values from -0.125 to 0.125
- state_matrix: bfloat16 [2048, 128], P('row', 'col'), may hold values from -0.125 to 0.125
- step_matrix: bfloat16 [2048, 64], P('row', 'col'), may hold values from -0.125 to 0.125
- channel_conv_taps: float32 [4, 4096], P(None, 'col'), may hold values from -3 to 3
- channel_conv_bias: float32 [4096], P('col'), may hold values from -3 to 3
- state_conv_taps: float32 [4, 128], P(None, 'col'), may hold values from -3 to 3
- state_conv_bias: float32 [128], P('col'), may hold values from -3 to 3
- step_size_bias: float32 [64], P('col'), may hold values from -6 to -1
- head_decay_logarithm: float32 [64], P('col'), may hold values from -0.5 to 2.5
- direct_head_scale: float32 [64], P('col'), may hold values from 0.5 to 1.5
- gated_norm_gain: float32 [4096], P('col'), may hold values from 0.5 to 1.5
- mixer_output_matrix: bfloat16 [4096, 2048], P('col', 'row'), may hold values from -0.09375 to 0.09375
- cotangent: bfloat16 [1024, 2048], P('row', 'col'), may hold values from -6 to 6
Outputs:
- block_output: bfloat16 [1024, 2048], P('row', 'col')
- grad_hidden: float32 [1024, 2048], P('row', 'col')
- grad_embeddings: float32 [1024, 2048], P('row', 'col')
- gradient_attention_gain: float32 [2, 2048], P(None, 'col')
- gradient_query_matrix: float32 [2, 2048, 4096], P(None, 'row', 'col')
- gradient_key_matrix: float32 [2, 2048, 4096], P(None, 'row', 'col')
- gradient_value_matrix: float32 [2, 2048, 4096], P(None, 'row', 'col')
- gradient_output_matrix: float32 [4096, 2, 2048], P('col', None, 'row')
- gradient_feedforward_gain: float32 [2, 2048], P(None, 'col')
- gradient_gate_matrix: float32 [2, 2048, 8192], P(None, 'row', 'col')
- gradient_up_matrix: float32 [2, 2048, 8192], P(None, 'row', 'col')
- gradient_adapter_down: float32 [2, 2048, 128], P(None, 'row', 'col')
- gradient_adapter_gate: float32 [128, 8192], P('row', 'col')
- gradient_adapter_up: float32 [128, 8192], P('row', 'col')
- gradient_down_matrix: float32 [8192, 2, 2048], P('col', None, 'row')
- gradient_projection_matrix: float32 [2, 2048, 2048], P(None, 'col', 'row')
- gradient_mixer_norm_gain: float32 [2048], P('col')
- gradient_mixer_gate_matrix: float32 [2048, 4096], P('row', 'col')
- gradient_mixer_input_matrix: float32 [2048, 4096], P('row', 'col')
- gradient_state_matrix: float32 [2048, 128], P('row', 'col')
- gradient_step_matrix: float32 [2048, 64], P('row', 'col')
- gradient_channel_taps: float32 [4, 4096], P(None, 'col')
- gradient_channel_bias: float32 [4096], P('col')
- gradient_state_taps: float32 [4, 128], P(None, 'col')
- gradient_state_bias: float32 [128], P('col')
- gradient_step_bias: float32 [64], P('col')
- gradient_decay_logarithm: float32 [64], P('col')
- gradient_direct_scale: float32 [64], P('col')
- gradient_gated_norm_gain: float32 [4096], P('col')
- gradient_mixer_output_matrix: float32 [4096, 2048], P('col', 'row')
The draws below stay inside these ranges and needn't reach their ends.
Inputs may be any that keep to these rules, and one draw needn't show every extreme that they name: `sequence_numbers`: within each block sequences are numbered from 0 in order, each of 4 sequences 1 to 128 tokens long, one exactly 128.
All inputs are finite; a program needn't handle non-finite values.
Results may differ from the reference program's by a relative error of at most 0.04.
Values may be sent and summed in bfloat16 or wider, within the bound.
No kernel may reach another device: no remote copies, remote signals or barrier semaphores. Data moves between devices by JAX's collectives and lax.ppermute only.
A program may use at most 256 MiB of HBM per device.

```python
import math
import jax
import jax.numpy as jnp
import numpy as np
from jax import lax

MODEL_WIDTH = 2048
HEADS = 32
HEAD = 128
FEEDFORWARD_UNITS = 8192
ADAPTER_RANK = 128
MHEADS = 64
NS = 64
KW = 4
DI = 4096
BLK = 256
SEQ_MAX = 128
SEGS = 4
NBLK = 4
TOKENS = 1024


def block_scale(rng, extent, split, least, largest):
    factor_of, own = 1.0, jax.random.fold_in(rng, 6)
    for axis_at, blocks in split:
        steps = jnp.exp(jax.random.uniform(jax.random.fold_in(own, axis_at), (blocks,), jnp.float32, least / len(split), largest / len(split)))
        factor_of = factor_of * jnp.repeat(steps, extent[axis_at] // blocks).reshape([-1 if axis == axis_at else 1 for axis in range(len(extent))])
    return factor_of


def split_up(count, total, limit, skew):
    loads = [(1 << 20) // math.isqrt(rank ** skew) + 1 for rank in range(2, count + 1)]
    surplus, given = total - limit - (count - 1), [1] * (count - 1)
    while surplus > 0:
        free = [i for i in range(count - 1) if given[i] < limit]
        pool, budget = sum([loads[i] for i in free]), surplus
        for i in free:
            more = min(limit - given[i], max(1, budget * loads[i] // pool), surplus)
            given[i] = given[i] + more
            surplus = surplus - more
    return np.array([limit] + given)


def ragged_sizes(rng, count, total, limit, slope):
    if count == 2:
        one = jax.random.randint(rng, (), max(1, total - limit), min(limit, total - 1) + 1)
        return jnp.stack([one, total - one])
    tallies = jnp.asarray(split_up(count, total, limit, slope), jnp.int32)
    couples = (count - 1) // 2
    donor, receiver = tallies[1:1 + 2 * couples:2], tallies[2:2 + 2 * couples:2]
    room = jnp.minimum(donor - 1, limit - receiver)
    passed = jax.random.randint(jax.random.fold_in(rng, 1), (couples,), 0, 1 << 20) % (room + 1)
    tallies = tallies.at[1:1 + 2 * couples:2].set(donor - passed).at[2:2 + 2 * couples:2].set(receiver + passed)
    return tallies[jax.random.permutation(jax.random.fold_in(rng, 2), count)]


def bell_draw(stream_key, dims, scale, limit, cuts=(), kind=jnp.bfloat16):
    factor_of = block_scale(stream_key, dims, cuts, -0.22, 0.18) if cuts else 1.0
    entries = jax.random.normal(stream_key, dims, jnp.float32) * scale * factor_of
    return jnp.minimum(jnp.maximum(entries, -limit), limit).astype(kind)


def setup_inputs(seed: int = 0) -> dict:
    arg_keys = jax.random.split(jax.random.key(seed), 32)
    return {
        "residual_input": bell_draw(arg_keys[0], (TOKENS, MODEL_WIDTH), 1.0, 6.0, ((0, 4), (1, 8))),
        "embeddings": bell_draw(arg_keys[1], (TOKENS, MODEL_WIDTH), 1.0, 6.0, ((0, 4), (1, 8))),
        "sequence_numbers": jax.vmap(lambda own: jnp.searchsorted(jnp.cumsum(ragged_sizes(own, SEGS, BLK, SEQ_MAX, 0)), jnp.arange(BLK), side="right"))(jax.random.split(arg_keys[2], NBLK)).reshape((NBLK, BLK)).astype(jnp.int32),
        "attention_norm_gain": jnp.clip(1.0 + 0.1 * jax.random.normal(arg_keys[3], (2, MODEL_WIDTH), jnp.float32), 0.5, 1.5),
        "query_matrix": bell_draw(arg_keys[4], (2, MODEL_WIDTH, 2 * MODEL_WIDTH), (2 * MODEL_WIDTH) ** -0.5, 0.09375, ((1, 4), (2, 8))),
        "key_matrix": bell_draw(arg_keys[5], (2, MODEL_WIDTH, 2 * MODEL_WIDTH), (2 * MODEL_WIDTH) ** -0.5, 0.09375, ((1, 4), (2, 8))),
        "value_matrix": bell_draw(arg_keys[6], (2, MODEL_WIDTH, 2 * MODEL_WIDTH), (2 * MODEL_WIDTH) ** -0.5, 0.09375, ((1, 4), (2, 8))),
        "attention_output_matrix": bell_draw(arg_keys[7], (2 * MODEL_WIDTH, 2, MODEL_WIDTH), (MODEL_WIDTH // 2) ** -0.5, 0.1875, ((0, 8), (2, 4))),
        "feedforward_norm_gain": jnp.clip(1.0 + 0.1 * jax.random.normal(arg_keys[8], (2, MODEL_WIDTH), jnp.float32), 0.5, 1.5),
        "gate_matrix": bell_draw(arg_keys[9], (2, MODEL_WIDTH, FEEDFORWARD_UNITS), (2 * MODEL_WIDTH) ** -0.5, 0.09375, ((1, 4), (2, 8))),
        "up_matrix": bell_draw(arg_keys[10], (2, MODEL_WIDTH, FEEDFORWARD_UNITS), (2 * MODEL_WIDTH) ** -0.5, 0.09375, ((1, 4), (2, 8))),
        "adapter_down": bell_draw(arg_keys[11], (2, MODEL_WIDTH, ADAPTER_RANK), (2 * MODEL_WIDTH) ** -0.5, 0.09375, ((1, 4), (2, 8))),
        "adapter_gate": bell_draw(arg_keys[12], (ADAPTER_RANK, FEEDFORWARD_UNITS), ADAPTER_RANK ** -0.5, 0.5, ((0, 4), (1, 8))),
        "adapter_up": bell_draw(arg_keys[13], (ADAPTER_RANK, FEEDFORWARD_UNITS), ADAPTER_RANK ** -0.5, 0.5, ((0, 4), (1, 8))),
        "down_matrix": bell_draw(arg_keys[14], (FEEDFORWARD_UNITS, 2, MODEL_WIDTH), FEEDFORWARD_UNITS ** -0.5, 0.0625, ((0, 8), (2, 4))),
        "projection_matrix": bell_draw(arg_keys[15], (2, MODEL_WIDTH, MODEL_WIDTH), (2 * MODEL_WIDTH) ** -0.5, 0.09375, ((1, 8), (2, 4))),
        "mixer_norm_gain": jnp.clip(1.0 + 0.1 * jax.random.normal(arg_keys[16], (MODEL_WIDTH,), jnp.float32), 0.5, 1.5),
        "mixer_gate_matrix": bell_draw(arg_keys[17], (MODEL_WIDTH, DI), MODEL_WIDTH ** -0.5, 0.125, ((0, 4), (1, 8))),
        "mixer_input_matrix": bell_draw(arg_keys[18], (MODEL_WIDTH, DI), MODEL_WIDTH ** -0.5, 0.125, ((0, 4), (1, 8))),
        "state_matrix": bell_draw(arg_keys[19], (MODEL_WIDTH, 2 * NS), MODEL_WIDTH ** -0.5, 0.125, ((0, 4), (1, 8))),
        "step_matrix": bell_draw(arg_keys[20], (MODEL_WIDTH, MHEADS), MODEL_WIDTH ** -0.5, 0.125, ((0, 4), (1, 8))),
        "channel_conv_taps": bell_draw(arg_keys[21], (KW, DI), KW ** -0.5, 3.0, ((1, 8),), jnp.float32),
        "channel_conv_bias": bell_draw(arg_keys[22], (DI,), 0.5, 3.0, ((0, 8),), jnp.float32),
        "state_conv_taps": bell_draw(arg_keys[23], (KW, 2 * NS), KW ** -0.5, 3.0, ((1, 8),), jnp.float32),
        "state_conv_bias": bell_draw(arg_keys[24], (2 * NS,), 0.5, 3.0, ((0, 8),), jnp.float32),
        "step_size_bias": jnp.clip(-6.0 + 5.0 * jax.random.uniform(arg_keys[25], (MHEADS,), jnp.float32) ** block_scale(arg_keys[25], (MHEADS,), ((0, 8),), -0.2, 0.2), -6.0, -1.0),
        "head_decay_logarithm": jnp.clip(-0.5 + 3.0 * jax.random.uniform(arg_keys[26], (MHEADS,), jnp.float32) ** block_scale(arg_keys[26], (MHEADS,), ((0, 8),), -0.2, 0.2), -0.5, 2.5),
        "direct_head_scale": jnp.clip(0.5 + 1.0 * jax.random.uniform(arg_keys[27], (MHEADS,), jnp.float32) ** block_scale(arg_keys[27], (MHEADS,), ((0, 8),), -0.2, 0.2), 0.5, 1.5),
        "gated_norm_gain": jnp.clip(1.0 + 0.1 * jax.random.normal(arg_keys[28], (DI,), jnp.float32), 0.5, 1.5),
        "mixer_output_matrix": bell_draw(arg_keys[29], (DI, MODEL_WIDTH), DI ** -0.5, 0.09375, ((0, 8), (1, 4))),
        "cotangent": bell_draw(arg_keys[30], (TOKENS, MODEL_WIDTH), 1.0, 6.0, ((0, 4), (1, 8))),
    }


epsilon = 1e-05
rope_base = 10000.0
highest = lax.Precision.HIGHEST
root_half = 0.7071067811865476
gauss_norm = 0.3989422804014327

def matrix_product(operand, other):
    return jnp.dot(operand, other, preferred_element_type=jnp.float32)

def matrix_product_left_transposed(operand, other):
    return jnp.dot(operand.T, other, preferred_element_type=jnp.float32)

def matrix_product_right_transposed(operand, other):
    return jnp.dot(operand, other.T, preferred_element_type=jnp.float32)

def norm_forward(stream, gain):
    factor = lax.rsqrt(lax.optimization_barrier(jnp.mean(stream * stream, axis=1, keepdims=True)) + epsilon)
    return ((stream * factor * gain).astype(jnp.bfloat16), factor)

def norm_backward(grad_out, stream, factor, gain):
    weighted = grad_out * gain
    projection = lax.optimization_barrier(jnp.mean(weighted * stream, axis=1, keepdims=True))
    grad_in = factor * weighted - stream * factor * factor * factor * projection
    return (grad_in, lax.optimization_barrier(jnp.sum(grad_out * stream * factor, axis=0)))

def positions_of(segments):
    indices = lax.broadcasted_iota(jnp.int32, segments.shape, 1)
    previous = jnp.concatenate([segments[:, :1] - 1, segments[:, :-1]], axis=1)
    starts = jnp.where(segments != previous, indices, 0)
    return indices - lax.cummax(starts, axis=1)

def visible(segments):
    length = segments.shape[1]
    query_index = lax.broadcasted_iota(jnp.int32, (length, length), 0)
    key_index = lax.broadcasted_iota(jnp.int32, (length, length), 1)
    same_segment = segments[:, :, None] == segments[:, None, :]
    return same_segment & (query_index >= key_index)[None]

def rope_tables(positions, head_size):
    half_size = head_size // 2
    frequency = jnp.exp(lax.broadcasted_iota(jnp.float32, (half_size,), 0) * (-2.0 * math.log(rope_base) / head_size))
    angles = positions.astype(jnp.float32)[..., None] * frequency
    return (jnp.cos(angles)[:, :, None, :], jnp.sin(angles)[:, :, None, :])

def rotate(heads, cosine, sine):
    half_size = heads.shape[-1] // 2
    first_half = heads[..., :half_size]
    second_half = heads[..., half_size:]
    return jnp.concatenate([first_half * cosine - second_half * sine, second_half * cosine + first_half * sine], axis=-1)

def rotate_back(gradient_list, cosine, sine):
    half_size = gradient_list.shape[-1] // 2
    first_half = gradient_list[..., :half_size]
    second_half = gradient_list[..., half_size:]
    return jnp.concatenate([first_half * cosine + second_half * sine, second_half * cosine - first_half * sine], axis=-1)

def conv_masks(segments, width):
    length = segments.shape[1]
    lag_masks = []
    for backstep in range(width):
        earlier = jnp.pad(segments, ((0, 0), (backstep, 0)), constant_values=-1)[:, :length]
        lag_masks.append((earlier == segments).astype(jnp.float32)[:, :, None])
    return lag_masks

def shift_down(shaped, amount):
    length = shaped.shape[1]
    return jnp.pad(shaped, ((0, 0), (amount, 0), (0, 0)))[:, :length]

def shift_up(shaped, amount):
    return jnp.pad(shaped, ((0, 0), (0, amount), (0, 0)))[:, amount:]

def silu_slope(preact, sigmoid_v):
    return sigmoid_v * (1.0 + preact * (1.0 - sigmoid_v))

def conv_pre(columns, kernel, offset, lag_masks):
    shaped = columns.reshape(lag_masks[0].shape[0], lag_masks[0].shape[1], -1)
    width = kernel.shape[0]
    running = jnp.zeros_like(shaped) + offset
    for backstep in range(width):
        running = running + kernel[width - 1 - backstep] * shift_down(shaped, backstep) * lag_masks[backstep]
    return running

def conv_forward(columns, kernel, offset, lag_masks):
    preact = conv_pre(columns, kernel, offset, lag_masks)
    return (preact * jax.nn.sigmoid(preact)).reshape(columns.shape)

def conv_backward(columns, kernel, offset, lag_masks, grad_act):
    preact = conv_pre(columns, kernel, offset, lag_masks)
    grad_pre = grad_act.reshape(preact.shape) * silu_slope(preact, jax.nn.sigmoid(preact))
    shaped = columns.reshape(preact.shape)
    width = kernel.shape[0]
    grad_columns = jnp.zeros_like(preact)
    kernel_rows = []
    for backstep in range(width):
        masked = grad_pre * lag_masks[backstep]
        grad_columns = grad_columns + shift_up(masked, backstep) * kernel[width - 1 - backstep]
        kernel_rows.append(lax.optimization_barrier(jnp.sum(masked * shift_down(shaped, backstep), axis=(0, 1))))
    return (grad_columns.reshape(columns.shape), jnp.stack(kernel_rows[::-1]), lax.optimization_barrier(jnp.sum(grad_pre, axis=(0, 1))))

def attend(queries, key_heads, values, allowed):
    factor = queries.shape[-1] ** (-0.5)
    scores = jnp.einsum('bqhd,bkhd->bhqk', queries.astype(jnp.float32), key_heads.astype(jnp.float32)) * factor
    scores = jnp.where(allowed[:, None], scores, -1e+30)
    highest_score = lax.optimization_barrier(jnp.max(scores, axis=-1, keepdims=True))
    logsum = highest_score + jnp.log(lax.optimization_barrier(jnp.sum(jnp.exp(scores - highest_score), axis=-1, keepdims=True)))
    probability = jnp.exp(scores - logsum).astype(jnp.bfloat16)
    attended = jnp.einsum('bhqk,bkhd->bqhd', probability.astype(jnp.float32), values.astype(jnp.float32))
    return (attended.astype(jnp.bfloat16), logsum)

def attend_back(queries, key_heads, values, logsum, allowed, grad_attended):
    factor = queries.shape[-1] ** (-0.5)
    scores = jnp.einsum('bqhd,bkhd->bhqk', queries.astype(jnp.float32), key_heads.astype(jnp.float32)) * factor
    scores = jnp.where(allowed[:, None], scores, -1e+30)
    exact_prob = jnp.exp(scores - logsum)
    probability = exact_prob.astype(jnp.bfloat16)
    grad_values = jnp.einsum('bhqk,bqhd->bkhd', probability.astype(jnp.float32), grad_attended.astype(jnp.float32))
    grad_prob = jnp.einsum('bqhd,bkhd->bhqk', grad_attended.astype(jnp.float32), values.astype(jnp.float32))
    row_total = lax.optimization_barrier(jnp.sum(exact_prob * grad_prob, axis=-1, keepdims=True))
    grad_scores = (exact_prob * (grad_prob - row_total) * factor).astype(jnp.bfloat16)
    grad_queries = jnp.einsum('bhqk,bkhd->bqhd', grad_scores.astype(jnp.float32), key_heads.astype(jnp.float32))
    grad_keys = jnp.einsum('bhqk,bqhd->bkhd', grad_scores.astype(jnp.float32), queries.astype(jnp.float32))
    return (grad_queries, grad_keys, grad_values)

def ssd_parts(inner_act, input_states, output_states, step_size, decay_rate, allowed):
    cumul = jnp.cumsum(step_size * decay_rate, axis=1)
    rising = jnp.transpose(cumul, (0, 2, 1))
    log_gap = rising[:, :, :, None] - rising[:, :, None, :]
    open_mask = allowed[:, None]
    decay_mat = jnp.where(open_mask, jnp.exp(jnp.where(open_mask, log_gap, 0.0)), 0.0)
    intersection = jnp.einsum('btn,bsn->bts', output_states.astype(jnp.float32), input_states.astype(jnp.float32), precision=highest)
    weighted = inner_act.astype(jnp.float32) * step_size[..., None]
    mixing = decay_mat * intersection[:, None]
    return (decay_mat, intersection, weighted, mixing)

def ssd_forward(inner_act, input_states, output_states, step_size, decay_rate, direct_head_scale, allowed):
    decay_mat, intersection, weighted, mixing = ssd_parts(inner_act, input_states, output_states, step_size, decay_rate, allowed)
    direct = direct_head_scale[:, None] * inner_act.astype(jnp.float32)
    return jnp.einsum('bhts,bshp->bthp', mixing, weighted, precision=highest) + direct

def ssd_backward(inner_act, input_states, output_states, step_size, decay_rate, direct_head_scale, allowed, grad_out):
    decay_mat, intersection, weighted, mixing = ssd_parts(inner_act, input_states, output_states, step_size, decay_rate, allowed)
    inner_wide = inner_act.astype(jnp.float32)
    grad_skip = lax.optimization_barrier(jnp.sum(grad_out * inner_wide, axis=(0, 1, 3)))
    grad_weighted = jnp.einsum('bhts,bthp->bshp', mixing, grad_out, precision=highest)
    grad_inner = grad_weighted * step_size[..., None] + direct_head_scale[:, None] * grad_out
    grad_step = lax.optimization_barrier(jnp.sum(grad_weighted * inner_wide, axis=-1))
    grad_mixing = jnp.einsum('bthp,bshp->bhts', grad_out, weighted, precision=highest)
    grad_intersection = lax.optimization_barrier(jnp.sum(grad_mixing * decay_mat, axis=1))
    grad_gap = grad_mixing * mixing
    grad_cumul = lax.optimization_barrier(jnp.sum(grad_gap, axis=3)) - lax.optimization_barrier(jnp.sum(grad_gap, axis=2))
    grad_rise = jnp.flip(jnp.cumsum(jnp.flip(grad_cumul, axis=-1), axis=-1), axis=-1)
    grad_rise = jnp.transpose(grad_rise, (0, 2, 1))
    grad_step = grad_step + grad_rise * decay_rate
    grad_rate = lax.optimization_barrier(jnp.sum(grad_rise * step_size, axis=(0, 1)))
    grad_output_states = jnp.einsum('bts,bsn->btn', grad_intersection, input_states.astype(jnp.float32), precision=highest)
    grad_input_states = jnp.einsum('bts,btn->bsn', grad_intersection, output_states.astype(jnp.float32), precision=highest)
    return (grad_inner, grad_step, grad_rate, grad_input_states, grad_output_states, grad_skip)

def block_pass(hidden, embedding, segments, cotangent_block, weight_list):
    attention_norm_gain, query_matrix_whole, key_matrix_whole, value_matrix_whole, output_matrix_whole, feedforward_norm_gain, gate_weight_whole, up_matrix_whole, adapter_down_whole, adapter_gate_whole, adapter_up_whole, down_weight_whole, projection_whole, mixer_norm_gain, mixer_gate_whole, mixer_input_whole, state_matrix_whole, step_matrix_whole, channel_conv_taps, channel_conv_bias, state_conv_taps, state_conv_bias, step_size_bias, head_decay_logarithm, direct_head_scale, gated_norm_gain, mixer_output_whole = weight_list
    tokens = hidden.shape[0]
    positions = positions_of(segments)
    allowed = visible(segments)
    cosine, sine = rope_tables(positions, HEAD)
    lag_masks = conv_masks(segments, KW)
    stream = jnp.concatenate([hidden, embedding], axis=1).astype(jnp.float32)
    normed_one, scale_one = norm_forward(stream, attention_norm_gain)
    heads_shape = (1, tokens, HEADS, HEAD)
    queries = rotate(matrix_product(normed_one, query_matrix_whole).reshape(heads_shape), cosine, sine).astype(jnp.bfloat16)
    key_heads = rotate(matrix_product(normed_one, key_matrix_whole).reshape(heads_shape), cosine, sine).astype(jnp.bfloat16)
    values = matrix_product(normed_one, value_matrix_whole).reshape(heads_shape).astype(jnp.bfloat16)
    attended, logsum = attend(queries, key_heads, values, allowed)
    attended_flat = attended.reshape(tokens, -1)
    after_attn = stream + matrix_product(attended_flat, output_matrix_whole)
    second_normalized, scale_two = norm_forward(after_attn, feedforward_norm_gain)
    adapter_middle = matrix_product(second_normalized, adapter_down_whole).astype(jnp.bfloat16)
    gate_preactivation = matrix_product(second_normalized, gate_weight_whole) + matrix_product(adapter_middle, adapter_gate_whole)
    up_preactivation = matrix_product(second_normalized, up_matrix_whole) + matrix_product(adapter_middle, adapter_up_whole)
    activated = jax.nn.gelu(gate_preactivation, approximate=False)
    hidden_mid = (activated * up_preactivation).astype(jnp.bfloat16)
    after_mlp = after_attn + matrix_product(hidden_mid, down_weight_whole)
    mlp_round = after_mlp.astype(jnp.bfloat16)
    mixed_in = hidden.astype(jnp.float32) + matrix_product(mlp_round, projection_whole)
    normed_three, scale_three = norm_forward(mixed_in, mixer_norm_gain)
    zgate = matrix_product(normed_three, mixer_gate_whole)
    inner_pre = matrix_product(normed_three, mixer_input_whole)
    state_pre = matrix_product(normed_three, state_matrix_whole)
    step_pre = matrix_product(normed_three, step_matrix_whole)
    inner_act = conv_forward(inner_pre, channel_conv_taps, channel_conv_bias, lag_masks).astype(jnp.bfloat16)
    states = conv_forward(state_pre, state_conv_taps, state_conv_bias, lag_masks).astype(jnp.bfloat16)
    input_states = states[:, :NS].reshape(1, tokens, NS)
    output_states = states[:, NS:].reshape(1, tokens, NS)
    step_size = jax.nn.softplus(step_pre + step_size_bias)
    decay_rate = -jnp.exp(head_decay_logarithm)
    mixer_heads = head_decay_logarithm.shape[0]
    inner_heads = inner_act.reshape(1, tokens, mixer_heads, -1)
    step_heads = step_size.reshape(1, tokens, mixer_heads)
    ssd_flat = ssd_forward(inner_heads, input_states, output_states, step_heads, decay_rate, direct_head_scale, allowed).reshape(tokens, -1)
    sigmoid_z = jax.nn.sigmoid(zgate)
    gated = ssd_flat * zgate * sigmoid_z
    normed_four, scale_four = norm_forward(gated, gated_norm_gain)
    block_out = (mixed_in + matrix_product(normed_four, mixer_output_whole)).astype(jnp.bfloat16)
    gradient_mixer_output_matrix = matrix_product_left_transposed(normed_four, cotangent_block)
    grad_normed_four = matrix_product_right_transposed(cotangent_block, mixer_output_whole)
    grad_gated, gradient_gated_norm_gain = norm_backward(grad_normed_four, gated, scale_four, gated_norm_gain)
    grad_ssd = grad_gated * zgate * sigmoid_z
    grad_zgate = grad_gated * ssd_flat * silu_slope(zgate, sigmoid_z)
    grad_inner, grad_step, grad_rate, grad_input_states, grad_output_states, gradient_direct_scale = ssd_backward(inner_heads, input_states, output_states, step_heads, decay_rate, direct_head_scale, allowed, grad_ssd.reshape(inner_heads.shape))
    grad_states = jnp.concatenate([grad_input_states, grad_output_states], axis=2).reshape(tokens, -1)
    grad_inner_pre, gradient_channel_taps, gradient_channel_bias = conv_backward(inner_pre, channel_conv_taps, channel_conv_bias, lag_masks, grad_inner.reshape(tokens, -1))
    grad_state_pre, gradient_state_taps, gradient_state_bias = conv_backward(state_pre, state_conv_taps, state_conv_bias, lag_masks, grad_states)
    grad_step_pre = grad_step.reshape(tokens, -1) * jax.nn.sigmoid(step_pre + step_size_bias)
    gradient_step_bias = lax.optimization_barrier(jnp.sum(grad_step_pre, axis=0))
    gradient_decay_logarithm = grad_rate * decay_rate
    round_zgate = grad_zgate.astype(jnp.bfloat16)
    round_inner = grad_inner_pre.astype(jnp.bfloat16)
    round_state = grad_state_pre.astype(jnp.bfloat16)
    round_step = grad_step_pre.astype(jnp.bfloat16)
    gradient_mixer_gate_matrix = matrix_product_left_transposed(normed_three, round_zgate)
    gradient_mixer_input_matrix = matrix_product_left_transposed(normed_three, round_inner)
    gradient_state_matrix = matrix_product_left_transposed(normed_three, round_state)
    gradient_step_matrix = matrix_product_left_transposed(normed_three, round_step)
    grad_normed_three = matrix_product_right_transposed(round_zgate, mixer_gate_whole) + matrix_product_right_transposed(round_inner, mixer_input_whole) + matrix_product_right_transposed(round_state, state_matrix_whole) + matrix_product_right_transposed(round_step, step_matrix_whole)
    grad_mixed_piece, gradient_mixer_norm_gain = norm_backward(grad_normed_three, mixed_in, scale_three, mixer_norm_gain)
    grad_mixed_in = cotangent_block.astype(jnp.float32) + grad_mixed_piece
    mixed_round = grad_mixed_in.astype(jnp.bfloat16)
    gradient_projection_matrix = matrix_product_left_transposed(mlp_round, mixed_round)
    grad_after_mlp = matrix_product_right_transposed(mixed_round, projection_whole)
    after_round = grad_after_mlp.astype(jnp.bfloat16)
    gradient_down_matrix = matrix_product_left_transposed(hidden_mid, after_round)
    grad_hidden_mid = matrix_product_right_transposed(after_round, down_weight_whole)
    cumulative = 0.5 * (1.0 + lax.erf(gate_preactivation * root_half))
    density = jnp.exp(-0.5 * gate_preactivation * gate_preactivation) * gauss_norm
    gradient_gate_preactivation = (grad_hidden_mid * up_preactivation * (cumulative + gate_preactivation * density)).astype(jnp.bfloat16)
    gradient_up_preactivation = (grad_hidden_mid * activated).astype(jnp.bfloat16)
    gradient_gate_matrix = matrix_product_left_transposed(second_normalized, gradient_gate_preactivation)
    gradient_up_matrix = matrix_product_left_transposed(second_normalized, gradient_up_preactivation)
    gradient_adapter_gate = matrix_product_left_transposed(adapter_middle, gradient_gate_preactivation)
    gradient_adapter_up = matrix_product_left_transposed(adapter_middle, gradient_up_preactivation)
    gradient_adapter_middle = (matrix_product_right_transposed(gradient_gate_preactivation, adapter_gate_whole) + matrix_product_right_transposed(gradient_up_preactivation, adapter_up_whole)).astype(jnp.bfloat16)
    gradient_adapter_down = matrix_product_left_transposed(second_normalized, gradient_adapter_middle)
    gradient_second_normalized = matrix_product_right_transposed(gradient_gate_preactivation, gate_weight_whole) + matrix_product_right_transposed(gradient_up_preactivation, up_matrix_whole) + matrix_product_right_transposed(gradient_adapter_middle, adapter_down_whole)
    grad_attn_piece, gradient_feedforward_gain = norm_backward(gradient_second_normalized, after_attn, scale_two, feedforward_norm_gain)
    grad_after_attn = grad_after_mlp + grad_attn_piece
    attn_round = grad_after_attn.astype(jnp.bfloat16)
    gradient_output_matrix = matrix_product_left_transposed(attended_flat, attn_round)
    grad_attended = matrix_product_right_transposed(attn_round, output_matrix_whole).astype(jnp.bfloat16).reshape(heads_shape)
    grad_queries, grad_keys, grad_values = attend_back(queries, key_heads, values, logsum, allowed, grad_attended)
    round_query = rotate_back(grad_queries, cosine, sine).reshape(tokens, -1).astype(jnp.bfloat16)
    round_key = rotate_back(grad_keys, cosine, sine).reshape(tokens, -1).astype(jnp.bfloat16)
    round_value = grad_values.reshape(tokens, -1).astype(jnp.bfloat16)
    gradient_query_matrix = matrix_product_left_transposed(normed_one, round_query)
    gradient_key_matrix = matrix_product_left_transposed(normed_one, round_key)
    gradient_value_matrix = matrix_product_left_transposed(normed_one, round_value)
    grad_normed_one = matrix_product_right_transposed(round_query, query_matrix_whole) + matrix_product_right_transposed(round_key, key_matrix_whole) + matrix_product_right_transposed(round_value, value_matrix_whole)
    grad_stream_piece, gradient_attention_gain = norm_backward(grad_normed_one, stream, scale_one, attention_norm_gain)
    grad_stream = grad_after_attn + grad_stream_piece
    model_width = hidden.shape[1]
    grad_hidden = grad_stream[:, :model_width] + grad_mixed_in
    grad_embedding = grad_stream[:, model_width:]
    gradient_list = (gradient_attention_gain, gradient_query_matrix, gradient_key_matrix, gradient_value_matrix, gradient_output_matrix, gradient_feedforward_gain, gradient_gate_matrix, gradient_up_matrix, gradient_adapter_down, gradient_adapter_gate, gradient_adapter_up, gradient_down_matrix, gradient_projection_matrix, gradient_mixer_norm_gain, gradient_mixer_gate_matrix, gradient_mixer_input_matrix, gradient_state_matrix, gradient_step_matrix, gradient_channel_taps, gradient_channel_bias, gradient_state_taps, gradient_state_bias, gradient_step_bias, gradient_decay_logarithm, gradient_direct_scale, gradient_gated_norm_gain, gradient_mixer_output_matrix)
    return (block_out, grad_hidden, grad_embedding, gradient_list)

def make_zero(template):
    return jnp.zeros(template.shape, jnp.float32)

def reference(residual_input, embeddings, sequence_numbers, attention_norm_gain, query_matrix, key_matrix, value_matrix, attention_output_matrix, feedforward_norm_gain, gate_matrix, up_matrix, adapter_down, adapter_gate, adapter_up, down_matrix, projection_matrix, mixer_norm_gain, mixer_gate_matrix, mixer_input_matrix, state_matrix, step_matrix, channel_conv_taps, channel_conv_bias, state_conv_taps, state_conv_bias, step_size_bias, head_decay_logarithm, direct_head_scale, gated_norm_gain, mixer_output_matrix, cotangent):
    block_count = sequence_numbers.shape[0]
    model_width = residual_input.shape[1]
    joined_width = 2 * model_width
    weight_list = (attention_norm_gain.reshape(-1), query_matrix.reshape(joined_width, -1), key_matrix.reshape(joined_width, -1), value_matrix.reshape(joined_width, -1), attention_output_matrix.reshape(attention_output_matrix.shape[0], -1), feedforward_norm_gain.reshape(-1), gate_matrix.reshape(joined_width, -1), up_matrix.reshape(joined_width, -1), adapter_down.reshape(joined_width, -1), adapter_gate, adapter_up, down_matrix.reshape(down_matrix.shape[0], -1), projection_matrix.reshape(joined_width, -1), mixer_norm_gain, mixer_gate_matrix, mixer_input_matrix, state_matrix, step_matrix, channel_conv_taps, channel_conv_bias, state_conv_taps, state_conv_bias, step_size_bias, head_decay_logarithm, direct_head_scale, gated_norm_gain, mixer_output_matrix)
    starting_values = (attention_norm_gain, query_matrix, key_matrix, value_matrix, attention_output_matrix, feedforward_norm_gain, gate_matrix, up_matrix, adapter_down, adapter_gate, adapter_up, down_matrix, projection_matrix, mixer_norm_gain, mixer_gate_matrix, mixer_input_matrix, state_matrix, step_matrix, channel_conv_taps, channel_conv_bias, state_conv_taps, state_conv_bias, step_size_bias, head_decay_logarithm, direct_head_scale, gated_norm_gain, mixer_output_matrix)
    pieces = (residual_input.reshape(block_count, BLK, -1), embeddings.reshape(block_count, BLK, -1), sequence_numbers.reshape(block_count, 1, BLK), cotangent.reshape(block_count, BLK, -1))

    def one_block(totals, piece_set):
        block_out, grad_hidden, grad_embedding, gradient_list = block_pass(piece_set[0], piece_set[1], piece_set[2], piece_set[3], weight_list)
        return (jax.tree.map(jnp.add, totals, gradient_list), (block_out, grad_hidden, grad_embedding))
    totals, stacked = lax.scan(one_block, jax.tree.map(make_zero, weight_list), pieces)
    block_output = stacked[0].reshape(-1, model_width)
    grad_hidden = stacked[1].reshape(-1, model_width)
    grad_embeddings = stacked[2].reshape(-1, model_width)
    shaped = tuple((total.reshape(initial.shape) for total, initial in zip(totals, starting_values)))
    return (block_output, grad_hidden, grad_embeddings) + shaped
```

```python
import math

import jax
import jax.numpy as jnp
from jax import lax
from jax.sharding import PartitionSpec as P

HEAD = 128
NS = 64
KW = 4


epsilon = 1e-05
rope_base = 10000.0
highest = lax.Precision.HIGHEST
root_half = 0.7071067811865476
gauss_norm = 0.3989422804014327


def matrix_product(operand, other):
    return jnp.dot(operand, other, preferred_element_type=jnp.float32)


def matrix_product_left_transposed(operand, other):
    return lax.dot_general(
        operand, other, (((0,), (0,)), ((), ())), preferred_element_type=jnp.float32
    )


def matrix_product_right_transposed(operand, other):
    return lax.dot_general(
        operand, other, (((1,), (1,)), ((), ())), preferred_element_type=jnp.float32
    )


def row_count():
    return lax.axis_size("row")


def col_count():
    return lax.axis_size("col")


def lanes():
    return col_count() // row_count()


def exchange(value, target):
    rows, cols = row_count(), col_count()
    pairs = []
    for row in range(rows):
        for col in range(cols):
            to_row, to_col = target(row, col)
            pairs.append((row * cols + col, to_row * cols + to_col))
    return lax.ppermute(value, ("row", "col"), pairs)


def swap_row(value, step):
    return exchange(value, lambda row, col: (row ^ step, col))


def swap_col(value, step):
    return exchange(value, lambda row, col: (row, col ^ step))


def swap_grid(value):
    width = lanes()
    return exchange(value, lambda row, col: (col // width, row * width + col % width))


def total_rows(value):
    step = 1
    while step < row_count():
        value = value + swap_row(value, step)
        step *= 2
    return value


def total_cols(value):
    step = 1
    while step < col_count():
        value = value + swap_col(value, step)
        step *= 2
    return value


def group_of():
    return lax.axis_index("col") // lanes()


def lane_of():
    return lax.axis_index("col") % lanes()


def offset_of():
    return lax.axis_index("row") ^ group_of()


def pick(stacked, index):
    return lax.dynamic_index_in_dim(stacked, index, 0, keepdims=False)


def lane_order(value):
    width = lanes()
    shaped = value.reshape((width, -1) + value.shape[1:])
    lane = lane_of()
    step = 1
    while step < width:
        cut = shaped.reshape((width // (2 * step), 2, step) + shaped.shape[1:])
        turned = jnp.concatenate([cut[:, 1:], cut[:, :1]], axis=1)
        shaped = jnp.where((lane & step) > 0, turned, cut).reshape(shaped.shape)
        step *= 2
    return shaped.reshape(value.shape)


def gather_cols(value):
    width = lanes()
    arrived = [value] + [swap_col(value, step * width) for step in range(1, row_count())]
    pieces = []
    for block in arrived:
        pieces.append(block)
        for step in range(1, width):
            pieces.append(swap_col(block, step))
    return jnp.concatenate(pieces, axis=0).reshape((row_count(), -1) + value.shape[1:])


def gather_rows(value):
    return [value] + [swap_row(value, step) for step in range(1, row_count())]


def by_rows(gathered):
    offset = offset_of()
    return [pick(gathered, step ^ offset) for step in range(row_count())]


def scatter_rows(lefts, weight, right_transposed=False):
    product = matrix_product_right_transposed if right_transposed else matrix_product
    sent = [
        swap_row(product(lefts[step], weight).astype(jnp.bfloat16), step)
        for step in range(1, row_count())
    ]
    total = product(lefts[0], weight)
    for piece in sent:
        total = total + piece.astype(jnp.float32)
    return total


def scatter_cols(partial):
    rows, width = row_count(), lanes()
    offset = offset_of()
    shaped = partial.reshape(rows, width, -1, partial.shape[-1])
    own = shaped[:, 0].astype(jnp.float32)
    for step in range(1, width):
        own = own + swap_col(shaped[:, step].astype(jnp.bfloat16), step).astype(jnp.float32)
    total = pick(own, offset)
    for step in range(1, rows):
        block = pick(own, step ^ offset).astype(jnp.bfloat16)
        total = total + swap_col(block, step * width).astype(jnp.float32)
    return total


def to_tokens(value):
    width = lanes()
    moved = swap_grid(value)
    shaped = moved.reshape((width, -1) + value.shape[1:])
    pieces = [shaped[0]] + [swap_col(shaped[step], step) for step in range(1, width)]
    stacked = jnp.stack(pieces)
    lane = lane_of()
    ordered = [pick(stacked, step ^ lane) for step in range(width)]
    joined = jnp.stack(ordered, axis=2)
    return joined.reshape(joined.shape[0], -1)


def to_rows(value, halves):
    width = lanes()
    shaped = value.reshape(value.shape[0], halves, width, -1)
    lane = lane_of()
    pieces = [
        lax.dynamic_index_in_dim(shaped, step ^ lane, 2, keepdims=False) for step in range(width)
    ]
    pieces = [pieces[0]] + [swap_col(pieces[step], step) for step in range(1, width)]
    return swap_grid(jnp.concatenate(pieces, axis=0))


def spread_cols(value):
    gathered = gather_cols(value).reshape((col_count(),) + value.shape)
    col = lax.axis_index("col")
    return jnp.concatenate([pick(gathered, step ^ col) for step in range(col_count())], axis=0)


def spread_rows(value):
    stacked = jnp.stack(gather_rows(value))
    row = lax.axis_index("row")
    return jnp.concatenate([pick(stacked, step ^ row) for step in range(row_count())], axis=0)


def collect_cols(value):
    shaped = value.reshape((col_count(), -1) + value.shape[1:])
    col = lax.axis_index("col")
    total = pick(shaped, col)
    for step in range(1, col_count()):
        total = total + swap_col(pick(shaped, step ^ col), step)
    return total


def collect_rows(value):
    shaped = value.reshape((row_count(), -1) + value.shape[1:])
    row = lax.axis_index("row")
    total = pick(shaped, row)
    for step in range(1, row_count()):
        total = total + swap_row(pick(shaped, step ^ row), step)
    return total


def norm_factor(stream, feature_count):
    squares = total_rows(jnp.sum(stream * stream, axis=1))
    return lax.rsqrt(squares / feature_count + epsilon)[:, None]


def norm_backward(grad_out, stream, factor, gain, feature_count):
    weighted = grad_out * gain
    projection = (total_rows(jnp.sum(weighted * stream, axis=1)) / feature_count)[:, None]
    grad_in = factor * weighted - stream * (factor * factor * factor * projection)
    return (grad_in, jnp.sum(grad_out * (stream * factor), axis=0))


def gain_slice(gain):
    width = lanes()
    moved = swap_grid(gain)
    pieces = jnp.stack([moved] + [swap_col(moved, step) for step in range(1, width)])
    lane = lane_of()
    return jnp.stack([pick(pieces, step ^ lane) for step in range(width)], axis=1).reshape(-1)


def gain_home(value, halves):
    shaped = value.reshape(halves, lanes(), -1)
    mine = lax.dynamic_index_in_dim(shaped, lane_of(), 1, keepdims=False)
    return swap_grid(mine)


def positions_of(segments):
    indices = lax.broadcasted_iota(jnp.int32, segments.shape, 1)
    previous = jnp.concatenate([segments[:, :1] - 1, segments[:, :-1]], axis=1)
    starts = jnp.where(segments != previous, indices, 0)
    return indices - lax.cummax(starts, axis=1)


def visible(segments):
    length = segments.shape[1]
    query_index = lax.broadcasted_iota(jnp.int32, (length, length), 0)
    key_index = lax.broadcasted_iota(jnp.int32, (length, length), 1)
    same_segment = segments[:, :, None] == segments[:, None, :]
    return same_segment & (query_index >= key_index)[None]


def rope_tables(positions, head_size):
    half_size = head_size // 2
    frequency = jnp.exp(
        lax.broadcasted_iota(jnp.float32, (half_size,), 0)
        * (-2.0 * math.log(rope_base) / head_size)
    )
    angles = positions.astype(jnp.float32)[..., None] * frequency
    return (jnp.cos(angles)[:, :, None, :], jnp.sin(angles)[:, :, None, :])


def rotate(heads, cosine, sine):
    half_size = heads.shape[-1] // 2
    first_half = heads[..., :half_size]
    second_half = heads[..., half_size:]
    return jnp.concatenate(
        [first_half * cosine - second_half * sine, second_half * cosine + first_half * sine],
        axis=-1,
    )


def rotate_back(gradient_list, cosine, sine):
    half_size = gradient_list.shape[-1] // 2
    first_half = gradient_list[..., :half_size]
    second_half = gradient_list[..., half_size:]
    return jnp.concatenate(
        [first_half * cosine + second_half * sine, second_half * cosine - first_half * sine],
        axis=-1,
    )


def conv_masks(segments, width):
    length = segments.shape[1]
    lag_masks = []
    for backstep in range(width):
        earlier = jnp.pad(segments, ((0, 0), (backstep, 0)), constant_values=-1)[:, :length]
        lag_masks.append((earlier == segments).astype(jnp.float32)[:, :, None])
    return lag_masks


def shift_down(shaped, amount):
    length = shaped.shape[1]
    return jnp.pad(shaped, ((0, 0), (amount, 0), (0, 0)))[:, :length]


def shift_up(shaped, amount):
    return jnp.pad(shaped, ((0, 0), (0, amount), (0, 0)))[:, amount:]


def silu_slope(preact, sigmoid_v):
    return sigmoid_v * (1.0 + preact * (1.0 - sigmoid_v))


def conv_pre(columns, kernel, offset, lag_masks):
    shaped = columns.reshape(lag_masks[0].shape[0], lag_masks[0].shape[1], -1)
    width = kernel.shape[0]
    running = jnp.zeros_like(shaped) + offset
    for backstep in range(width):
        running = (
            running
            + kernel[width - 1 - backstep] * shift_down(shaped, backstep) * lag_masks[backstep]
        )
    return running


def conv_forward(columns, kernel, offset, lag_masks):
    preact = conv_pre(columns, kernel, offset, lag_masks)
    return (preact * jax.nn.sigmoid(preact)).reshape(columns.shape)


def conv_backward(columns, kernel, offset, lag_masks, grad_act):
    preact = conv_pre(columns, kernel, offset, lag_masks)
    grad_pre = grad_act.reshape(preact.shape) * silu_slope(preact, jax.nn.sigmoid(preact))
    shaped = columns.reshape(preact.shape)
    width = kernel.shape[0]
    grad_columns = jnp.zeros_like(preact)
    kernel_rows = []
    for backstep in range(width):
        masked = grad_pre * lag_masks[backstep]
        grad_columns = grad_columns + shift_up(masked, backstep) * kernel[width - 1 - backstep]
        kernel_rows.append(jnp.sum(masked * shift_down(shaped, backstep), axis=(0, 1)))
    return (
        grad_columns.reshape(columns.shape),
        jnp.stack(kernel_rows[::-1]),
        jnp.sum(grad_pre, axis=(0, 1)),
    )


def attend(queries, key_heads, values, allowed):
    factor = queries.shape[-1] ** (-0.5)
    scores = (
        jnp.einsum("bqhd,bkhd->bhqk", queries, key_heads, preferred_element_type=jnp.float32)
        * factor
    )
    scores = jnp.where(allowed[:, None], scores, -1e30)
    highest_score = jnp.max(scores, axis=-1, keepdims=True)
    logsum = highest_score + jnp.log(
        jnp.sum(jnp.exp(scores - highest_score), axis=-1, keepdims=True)
    )
    probability = jnp.exp(scores - logsum).astype(jnp.bfloat16)
    attended = jnp.einsum(
        "bhqk,bkhd->bqhd", probability, values, preferred_element_type=jnp.float32
    )
    return (attended.astype(jnp.bfloat16), logsum)


def attend_back(queries, key_heads, values, logsum, allowed, grad_attended):
    factor = queries.shape[-1] ** (-0.5)
    scores = (
        jnp.einsum("bqhd,bkhd->bhqk", queries, key_heads, preferred_element_type=jnp.float32)
        * factor
    )
    scores = jnp.where(allowed[:, None], scores, -1e30)
    exact_prob = jnp.exp(scores - logsum)
    probability = exact_prob.astype(jnp.bfloat16)
    grad_values = jnp.einsum(
        "bhqk,bqhd->bkhd", probability, grad_attended, preferred_element_type=jnp.float32
    )
    grad_prob = jnp.einsum(
        "bqhd,bkhd->bhqk", grad_attended, values, preferred_element_type=jnp.float32
    )
    row_total = jnp.sum(exact_prob * grad_prob, axis=-1, keepdims=True)
    grad_scores = (exact_prob * (grad_prob - row_total) * factor).astype(jnp.bfloat16)
    grad_queries = jnp.einsum(
        "bhqk,bkhd->bqhd", grad_scores, key_heads, preferred_element_type=jnp.float32
    )
    grad_keys = jnp.einsum(
        "bhqk,bqhd->bkhd", grad_scores, queries, preferred_element_type=jnp.float32
    )
    return (grad_queries, grad_keys, grad_values)


def ssd_parts(inner_act, input_states, output_states, step_size, decay_rate, allowed):
    cumul = jnp.cumsum(step_size * decay_rate, axis=1)
    rising = jnp.transpose(cumul, (0, 2, 1))
    log_gap = rising[:, :, :, None] - rising[:, :, None, :]
    open_mask = allowed[:, None]
    decay_mat = jnp.where(open_mask, jnp.exp(jnp.where(open_mask, log_gap, 0.0)), 0.0)
    intersection = jnp.einsum(
        "btn,bsn->bts",
        output_states.astype(jnp.float32),
        input_states.astype(jnp.float32),
        precision=highest,
    )
    weighted = inner_act.astype(jnp.float32) * step_size[..., None]
    mixing = decay_mat * intersection[:, None]
    return (decay_mat, intersection, weighted, mixing)


def ssd_forward(
    inner_act, input_states, output_states, step_size, decay_rate, direct_head_scale, allowed
):
    decay_mat, intersection, weighted, mixing = ssd_parts(
        inner_act, input_states, output_states, step_size, decay_rate, allowed
    )
    direct = direct_head_scale[:, None] * inner_act.astype(jnp.float32)
    return jnp.einsum("bhts,bshp->bthp", mixing, weighted, precision=highest) + direct


def ssd_backward(
    inner_act,
    input_states,
    output_states,
    step_size,
    decay_rate,
    direct_head_scale,
    allowed,
    grad_out,
):
    decay_mat, intersection, weighted, mixing = ssd_parts(
        inner_act, input_states, output_states, step_size, decay_rate, allowed
    )
    inner_wide = inner_act.astype(jnp.float32)
    grad_skip = jnp.sum(grad_out * inner_wide, axis=(0, 1, 3))
    grad_weighted = jnp.einsum("bhts,bthp->bshp", mixing, grad_out, precision=highest)
    grad_inner = grad_weighted * step_size[..., None] + direct_head_scale[:, None] * grad_out
    grad_step = jnp.sum(grad_weighted * inner_wide, axis=-1)
    grad_mixing = jnp.einsum("bthp,bshp->bhts", grad_out, weighted, precision=highest)
    grad_intersection = jnp.sum(grad_mixing * decay_mat, axis=1)
    grad_gap = grad_mixing * mixing
    grad_cumul = jnp.sum(grad_gap, axis=3) - jnp.sum(grad_gap, axis=2)
    grad_rise = jnp.flip(jnp.cumsum(jnp.flip(grad_cumul, axis=-1), axis=-1), axis=-1)
    grad_rise = jnp.transpose(grad_rise, (0, 2, 1))
    grad_step = grad_step + grad_rise * decay_rate
    grad_rate = jnp.sum(grad_rise * step_size, axis=(0, 1))
    grad_output_states = jnp.einsum(
        "bts,bsn->btn", grad_intersection, input_states.astype(jnp.float32), precision=highest
    )
    grad_input_states = jnp.einsum(
        "bts,btn->bsn", grad_intersection, output_states.astype(jnp.float32), precision=highest
    )
    return (grad_inner, grad_step, grad_rate, grad_input_states, grad_output_states, grad_skip)


def shards(
    residual_input,
    embeddings,
    sequence_numbers,
    attention_norm_gain,
    query_matrix,
    key_matrix,
    value_matrix,
    attention_output_matrix,
    feedforward_norm_gain,
    gate_matrix,
    up_matrix,
    adapter_down,
    adapter_gate,
    adapter_up,
    down_matrix,
    projection_matrix,
    mixer_norm_gain,
    mixer_gate_matrix,
    mixer_input_matrix,
    state_matrix,
    step_matrix,
    channel_conv_taps,
    channel_conv_bias,
    state_conv_taps,
    state_conv_bias,
    step_size_bias,
    head_decay_logarithm,
    direct_head_scale,
    gated_norm_gain,
    mixer_output_matrix,
    cotangent,
):
    blocks, block_length = sequence_numbers.shape
    token_rows, local_width = residual_input.shape
    model_width = local_width * col_count()
    joined_width = 2 * model_width
    inner_local = channel_conv_bias.shape[0]
    inner_width = inner_local * col_count()
    slice_width = local_width * lanes()
    bf16 = jnp.bfloat16
    positions = positions_of(sequence_numbers)
    allowed = visible(sequence_numbers)
    cosine, sine = rope_tables(positions, HEAD)
    lag_masks = conv_masks(sequence_numbers, KW)

    flat = lambda matrix: matrix.reshape(-1, matrix.shape[-1])
    attn_weight = jnp.concatenate([flat(query_matrix), flat(key_matrix), flat(value_matrix)], axis=1)
    output_weight = attention_output_matrix.reshape(attention_output_matrix.shape[0], -1)
    down_weight = down_matrix.reshape(down_matrix.shape[0], -1)
    project_weight = flat(projection_matrix)
    gains = jnp.concatenate([attention_norm_gain, feedforward_norm_gain, mixer_norm_gain[None]])

    stream_rows = lane_order(jnp.stack([residual_input, embeddings], axis=1))
    stream_bf = to_tokens(stream_rows)
    gain_all = gain_slice(gains).reshape(5, -1)
    gain_one = gain_all[:2].reshape(-1)
    gain_two = gain_all[2:4].reshape(-1)
    gain_three = gain_all[4]
    cot_bf = to_tokens(lane_order(cotangent[:, None]))
    stream = stream_bf.astype(jnp.float32)
    cot_tokens = cot_bf.astype(jnp.float32)
    residual = stream[:, :slice_width]

    scale_one = norm_factor(stream, joined_width)
    normed_one = (stream * scale_one * gain_one).astype(bf16)
    left_one = by_rows(gather_cols(normed_one))
    attn_pre = lane_order(scatter_rows(left_one, attn_weight))

    small_weight = jnp.concatenate([flat(adapter_down).T, state_matrix.T], axis=1)
    small_whole = spread_cols(small_weight)
    adapter_down_whole = small_whole[:, : joined_width // row_count()]
    state_whole = small_whole[:, joined_width // row_count() :]
    adapter_out = jnp.concatenate([adapter_gate, adapter_up], axis=1)
    adapter_out_whole = spread_rows(adapter_out)
    pair_weight = jnp.concatenate([flat(gate_matrix), flat(up_matrix)], axis=1)
    pair_weight = (
        pair_weight.astype(jnp.float32)
        + matrix_product_left_transposed(adapter_down_whole, adapter_out_whole)
    ).astype(bf16)
    state_conv = spread_cols(jnp.concatenate([state_conv_taps, state_conv_bias[None]]).T).T
    state_taps_whole, state_bias_whole = state_conv[:KW], state_conv[KW]
    state_width = state_whole.shape[0]
    step_width = step_matrix.shape[1]
    mixer_used = 2 * inner_local + state_width + step_width
    mixer_padding = -mixer_used % 128
    mixer_weight = jnp.concatenate(
        [
            mixer_gate_matrix,
            mixer_input_matrix,
            state_whole.T,
            step_matrix,
            jnp.zeros((step_matrix.shape[0], mixer_padding), bf16),
        ],
        axis=1,
    )

    left_cot = by_rows(gather_cols(cot_bf))
    grad_normed_four = lane_order(scatter_rows(left_cot, mixer_output_matrix, True))

    heads_here = attn_pre.shape[1] // (3 * HEAD)
    heads_shape = (blocks, block_length, heads_here, HEAD)
    part = heads_here * HEAD
    queries = rotate(attn_pre[:, :part].reshape(heads_shape), cosine, sine).astype(bf16)
    key_heads = rotate(attn_pre[:, part : 2 * part].reshape(heads_shape), cosine, sine).astype(bf16)
    values = attn_pre[:, 2 * part :].reshape(heads_shape).astype(bf16)
    attended, logsum = attend(queries, key_heads, values, allowed)
    attended_all = jnp.concatenate(gather_rows(lane_order(attended.reshape(token_rows, -1))), axis=0)
    after_attn = stream + scatter_cols(matrix_product(attended_all, output_weight))

    scale_two = norm_factor(after_attn, joined_width)
    normed_two = (after_attn * scale_two * gain_two).astype(bf16)
    gathered_two = gather_cols(normed_two)
    left_two = by_rows(gathered_two)
    pair_pre = lane_order(scatter_rows(left_two, pair_weight))
    hidden_width = pair_pre.shape[1] // 2
    gate_preactivation = pair_pre[:, :hidden_width]
    up_preactivation = pair_pre[:, hidden_width:]
    activated = jax.nn.gelu(gate_preactivation, approximate=False)
    hidden_mid = (activated * up_preactivation).astype(bf16)
    hidden_all = jnp.concatenate(gather_rows(lane_order(hidden_mid)), axis=0)
    after_mlp = after_attn + scatter_cols(matrix_product(hidden_all, down_weight))
    mlp_rows = to_rows(after_mlp.astype(bf16), 2)
    mlp_all = jnp.concatenate(gather_rows(mlp_rows.reshape(token_rows, -1)), axis=0)
    mixed_in = residual + scatter_cols(matrix_product(mlp_all, project_weight))

    scale_three = norm_factor(mixed_in, model_width)
    normed_three = (mixed_in * scale_three * gain_three).astype(bf16)
    left_three = by_rows(gather_cols(normed_three))
    mixer_pre = lane_order(scatter_rows(left_three, mixer_weight))
    zgate = mixer_pre[:, :inner_local]
    inner_pre = mixer_pre[:, inner_local : 2 * inner_local]
    state_pre = mixer_pre[:, 2 * inner_local : 2 * inner_local + state_width]
    step_pre = mixer_pre[:, 2 * inner_local + state_width : mixer_used]
    inner_act = conv_forward(inner_pre, channel_conv_taps, channel_conv_bias, lag_masks).astype(bf16)
    states = conv_forward(state_pre, state_taps_whole, state_bias_whole, lag_masks).astype(bf16)
    input_states = states[:, :NS].reshape(blocks, block_length, NS)
    output_states = states[:, NS:].reshape(blocks, block_length, NS)
    step_size = jax.nn.softplus(step_pre + step_size_bias)
    decay_rate = -jnp.exp(head_decay_logarithm)
    mixer_heads = head_decay_logarithm.shape[0]
    inner_heads = inner_act.reshape(blocks, block_length, mixer_heads, -1)
    step_heads = step_size.reshape(blocks, block_length, mixer_heads)
    ssd_flat = ssd_forward(
        inner_heads, input_states, output_states, step_heads, decay_rate, direct_head_scale, allowed
    ).reshape(token_rows, -1)
    sigmoid_z = jax.nn.sigmoid(zgate)
    gated = ssd_flat * zgate * sigmoid_z
    weighted_four = grad_normed_four * gated_norm_gain
    sums_four = total_cols(
        jnp.stack([jnp.sum(gated * gated, axis=1), jnp.sum(weighted_four * gated, axis=1)])
    )
    scale_four = lax.rsqrt(sums_four[0] / inner_width + epsilon)[:, None]
    projection_four = (sums_four[1] / inner_width)[:, None]
    grad_gated = scale_four * weighted_four - gated * (
        scale_four * scale_four * scale_four * projection_four
    )
    gradient_gated_norm_gain = jnp.sum(grad_normed_four * (gated * scale_four), axis=0)
    normed_four = (gated * scale_four * gated_norm_gain).astype(bf16)

    grad_ssd = grad_gated * zgate * sigmoid_z
    grad_zgate = grad_gated * ssd_flat * silu_slope(zgate, sigmoid_z)
    (
        grad_inner,
        grad_step,
        grad_rate,
        grad_input_states,
        grad_output_states,
        gradient_direct_scale,
    ) = ssd_backward(
        inner_heads,
        input_states,
        output_states,
        step_heads,
        decay_rate,
        direct_head_scale,
        allowed,
        grad_ssd.reshape(inner_heads.shape),
    )
    grad_states = jnp.concatenate([grad_input_states, grad_output_states], axis=2).reshape(
        token_rows, -1
    )
    grad_inner_pre, gradient_channel_taps, gradient_channel_bias = conv_backward(
        inner_pre,
        channel_conv_taps,
        channel_conv_bias,
        lag_masks,
        grad_inner.reshape(token_rows, -1),
    )
    grad_state_pre, gradient_state_taps, gradient_state_bias = conv_backward(
        state_pre, state_taps_whole, state_bias_whole, lag_masks, grad_states
    )
    grad_step_pre = grad_step.reshape(token_rows, -1) * jax.nn.sigmoid(step_pre + step_size_bias)
    gradient_step_bias = jnp.sum(grad_step_pre, axis=0)
    gradient_decay_logarithm = grad_rate * decay_rate
    mixer_grads = jnp.concatenate(
        [
            grad_zgate.astype(bf16),
            grad_inner_pre.astype(bf16),
            grad_state_pre.astype(bf16),
            grad_step_pre.astype(bf16),
            jnp.zeros((token_rows, mixer_padding), bf16),
        ],
        axis=1,
    )
    mixer_grads_all = jnp.concatenate(gather_rows(lane_order(mixer_grads)), axis=0)
    grad_normed_three = scatter_cols(matrix_product_right_transposed(mixer_grads_all, mixer_weight))
    grad_mixed_piece, gain_three_part = norm_backward(
        grad_normed_three, mixed_in, scale_three, gain_three, model_width
    )
    grad_mixed_in = cot_tokens + grad_mixed_piece

    normed_four_all = jnp.concatenate(gather_rows(lane_order(normed_four)), axis=0)
    block_tokens = mixed_in + scatter_cols(matrix_product(normed_four_all, mixer_output_matrix))
    block_output = lane_order(to_rows(block_tokens.astype(bf16), 1).reshape(token_rows, -1))
    join = lambda pieces: jnp.concatenate(pieces, axis=0)
    left_cot = join(left_cot)
    gradient_mixer_output_matrix = matrix_product_left_transposed(normed_four_all, left_cot)
    left_three = join(left_three)
    gradient_mixer_gate_matrix = matrix_product_left_transposed(
        left_three, mixer_grads_all[:, :inner_local]
    )
    gradient_mixer_input_matrix = matrix_product_left_transposed(
        left_three, mixer_grads_all[:, inner_local : 2 * inner_local]
    )
    small_grads = matrix_product_left_transposed(mixer_grads_all[:, 2 * inner_local :], left_three)
    gradient_state_matrix = collect_cols(small_grads[:state_width]).T
    gradient_step_matrix = small_grads[state_width : state_width + step_width].T

    left_mixed = by_rows(gather_cols(grad_mixed_in.astype(bf16)))
    grad_after_rows = scatter_rows(left_mixed, project_weight, True)
    after_round = to_tokens(grad_after_rows.astype(bf16).reshape(token_rows, 2, -1))
    grad_after_mlp = after_round.astype(jnp.float32)
    left_after = by_rows(gather_cols(after_round))
    grad_hidden_mid = lane_order(scatter_rows(left_after, down_weight, True))
    cumulative = 0.5 * (1.0 + lax.erf(gate_preactivation * root_half))
    density = jnp.exp(-0.5 * gate_preactivation * gate_preactivation) * gauss_norm
    pair_grads = jnp.concatenate(
        [
            (
                grad_hidden_mid * up_preactivation * (cumulative + gate_preactivation * density)
            ).astype(bf16),
            (grad_hidden_mid * activated).astype(bf16),
        ],
        axis=1,
    )
    pair_grads_all = jnp.concatenate(gather_rows(lane_order(pair_grads)), axis=0)
    grad_normed_two = scatter_cols(matrix_product_right_transposed(pair_grads_all, pair_weight))
    grad_attn_piece, gain_two_part = norm_backward(
        grad_normed_two, after_attn, scale_two, gain_two, joined_width
    )
    grad_after_attn = grad_after_mlp + grad_attn_piece

    left_mixed, left_after, left_two = join(left_mixed), join(left_after), join(left_two)
    gradient_projection_matrix = matrix_product_left_transposed(mlp_all, left_mixed)
    gradient_down_matrix = matrix_product_left_transposed(hidden_all, left_after)
    gate_grads_all = pair_grads_all[:, :hidden_width]
    up_grads_all = pair_grads_all[:, hidden_width:]
    gradient_gate_matrix = matrix_product_left_transposed(left_two, gate_grads_all)
    gradient_up_matrix = matrix_product_left_transposed(left_two, up_grads_all)
    middle = collect_rows(matrix_product_right_transposed(adapter_down_whole, flat(gathered_two)))
    middle = middle.astype(bf16).reshape(middle.shape[0], row_count(), -1)
    offset = offset_of()
    middle = jnp.concatenate(
        [
            lax.dynamic_index_in_dim(middle, step ^ offset, 1, keepdims=False)
            for step in range(row_count())
        ],
        axis=1,
    )
    gradient_adapter_gate = matrix_product(middle, gate_grads_all)
    gradient_adapter_up = matrix_product(middle, up_grads_all)
    grad_middle = collect_cols(matrix_product_right_transposed(adapter_out_whole, pair_grads))
    grad_middle = jnp.concatenate(gather_rows(lane_order(grad_middle.astype(bf16).T)), axis=0)
    gradient_adapter_down = matrix_product_left_transposed(left_two, grad_middle)

    left_attn = by_rows(gather_cols(grad_after_attn.astype(bf16)))
    grad_attended = (
        lane_order(scatter_rows(left_attn, output_weight, True)).astype(bf16).reshape(heads_shape)
    )
    grad_queries, grad_keys, grad_values = attend_back(
        queries, key_heads, values, logsum, allowed, grad_attended
    )
    attn_grads = jnp.concatenate(
        [
            rotate_back(grad_queries, cosine, sine).reshape(token_rows, -1).astype(bf16),
            rotate_back(grad_keys, cosine, sine).reshape(token_rows, -1).astype(bf16),
            grad_values.reshape(token_rows, -1).astype(bf16),
        ],
        axis=1,
    )
    attn_grads_all = jnp.concatenate(gather_rows(lane_order(attn_grads)), axis=0)
    grad_normed_one = scatter_cols(matrix_product_right_transposed(attn_grads_all, attn_weight))
    grad_stream_piece, gain_one_part = norm_backward(
        grad_normed_one, stream, scale_one, gain_one, joined_width
    )
    grad_stream = grad_after_attn + grad_stream_piece
    grad_both = jnp.concatenate(
        [grad_stream[:, :slice_width] + grad_mixed_in, grad_stream[:, slice_width:]], axis=1
    )
    grad_out = lane_order(to_rows(grad_both.astype(bf16), 2)).astype(jnp.float32)
    grad_hidden = grad_out[:, 0]
    grad_embeddings = grad_out[:, 1]

    left_attn, left_one = join(left_attn), join(left_one)
    gradient_output_matrix = matrix_product_left_transposed(attended_all, left_attn)
    gradient_query_matrix = matrix_product_left_transposed(left_one, attn_grads_all[:, :part])
    gradient_key_matrix = matrix_product_left_transposed(
        left_one, attn_grads_all[:, part : 2 * part]
    )
    gradient_value_matrix = matrix_product_left_transposed(left_one, attn_grads_all[:, 2 * part :])

    gain_parts = jnp.concatenate([gain_one_part, gain_two_part, gain_three_part])
    gain_grads = gain_home(total_cols(gain_parts), 5)
    small_parts = (
        gradient_channel_taps.reshape(-1),
        gradient_channel_bias,
        gradient_gated_norm_gain,
        gradient_state_taps.reshape(-1),
        gradient_state_bias,
        gradient_step_bias,
        gradient_decay_logarithm,
        gradient_direct_scale,
    )
    small = total_rows(jnp.concatenate(small_parts))
    ends, at = [], 0
    for piece in small_parts:
        ends.append(small[at : at + piece.shape[0]])
        at += piece.shape[0]
    state_small = total_cols(jnp.concatenate(ends[3:5])).reshape(KW + 1, -1)
    state_here = state_conv_bias.shape[0]
    state_small = lax.dynamic_slice_in_dim(
        state_small, lax.axis_index("col") * state_here, state_here, axis=1
    )
    return (
        block_output,
        grad_hidden,
        grad_embeddings,
        gain_grads[:2],
        gradient_query_matrix.reshape(query_matrix.shape),
        gradient_key_matrix.reshape(key_matrix.shape),
        gradient_value_matrix.reshape(value_matrix.shape),
        gradient_output_matrix.reshape(attention_output_matrix.shape),
        gain_grads[2:4],
        gradient_gate_matrix.reshape(gate_matrix.shape),
        gradient_up_matrix.reshape(up_matrix.shape),
        gradient_adapter_down.reshape(adapter_down.shape),
        gradient_adapter_gate,
        gradient_adapter_up,
        gradient_down_matrix.reshape(down_matrix.shape),
        gradient_projection_matrix.reshape(projection_matrix.shape),
        gain_grads[4],
        gradient_mixer_gate_matrix,
        gradient_mixer_input_matrix,
        gradient_state_matrix,
        gradient_step_matrix,
        ends[0].reshape(channel_conv_taps.shape),
        ends[1],
        state_small[:KW],
        state_small[KW],
        ends[5],
        ends[6],
        ends[7],
        ends[2],
        gradient_mixer_output_matrix,
    )


def solution(mesh):
    placed = (
        P("row", "col"),
        P("row", "col"),
        P("row", None),
        P(None, "col"),
        P(None, "row", "col"),
        P(None, "row", "col"),
        P(None, "row", "col"),
        P("col", None, "row"),
        P(None, "col"),
        P(None, "row", "col"),
        P(None, "row", "col"),
        P(None, "row", "col"),
        P("row", "col"),
        P("row", "col"),
        P("col", None, "row"),
        P(None, "col", "row"),
        P("col"),
        P("row", "col"),
        P("row", "col"),
        P("row", "col"),
        P("row", "col"),
        P(None, "col"),
        P("col"),
        P(None, "col"),
        P("col"),
        P("col"),
        P("col"),
        P("col"),
        P("col"),
        P("col", "row"),
        P("row", "col"),
    )
    return jax.shard_map(
        shards,
        mesh=mesh,
        in_specs=placed,
        out_specs=(
            P("row", "col"),
            P("row", "col"),
            P("row", "col"),
            P(None, "col"),
            P(None, "row", "col"),
            P(None, "row", "col"),
            P(None, "row", "col"),
            P("col", None, "row"),
            P(None, "col"),
            P(None, "row", "col"),
            P(None, "row", "col"),
            P(None, "row", "col"),
            P("row", "col"),
            P("row", "col"),
            P("col", None, "row"),
            P(None, "col", "row"),
            P("col"),
            P("row", "col"),
            P("row", "col"),
            P("row", "col"),
            P("row", "col"),
            P(None, "col"),
            P("col"),
            P(None, "col"),
            P("col"),
            P("col"),
            P("col"),
            P("col"),
            P("col"),
            P("col", "row"),
        ),
        check_vma=False,
    )
```
